512 devices in a mesh: expert: 64 (over z, x), tensor: 8 (over y, core).
Axes of the slice: x: 4, y: 4, z: 16, core: 2. Of those that a mesh axis runs over, the one named last changes fastest.
Arguments:
- tokens: bfloat16 [8192, 7168], P('expert', 'tensor'), may hold values from -6 to 6
- route_ids: int32 [8192, 8], P('expert'), may hold values from 0 to 255, as said below
- route_weight: float32 [8192, 8], P('expert'), may hold values from 0.1 to 2.5
- gate_up: bfloat16 [64, 2, 7168, 1024], P('expert', None, None, 'tensor'), may hold values from -0.0625 to 0.0625
- block_keep: int32 [64, 2, 112, 16], P('expert', None, None, 'tensor'), may hold values 0 or 1
Outputs:
- hidden_slots: bfloat16 [64, 512, 1024], P('expert', None, 'tensor')
The draws below stay inside these ranges and needn't reach their ends.
Inputs may be any that keep to these rules, and one draw needn't show every extreme that they name: `route_ids`: each row names 8 different experts. Within each aligned block of 128 rows no expert is named by more than 8 rows, and one expert numbered below 64 is named by exactly 8 rows in every block.
All inputs are finite; a program needn't handle non-finite values. No bound on the sum of `block_keep` on one device may be relied on, other than what follows from the above.
Results may differ from the reference program's by a relative error of at most 0.0051.
Values may be sent and summed in bfloat16 or wider, within the bound.
A program may use at most 64 MiB of HBM per device.

```python
import jax
import jax.numpy as jnp
from jax import lax

D = 7168
EXPERTS = 256
TOP = 8
FF = 1024
BLOCK = 64
TOK_DEV = 128
CAP = 8
FLIGHT = 64
TOKENS = 8192
ROWS = 512


def draw_route_ids(key, part):
    block_count = TOKENS // TOK_DEV
    slot_total = EXPERTS * CAP
    popular_key = jax.random.fold_in(key, 11)
    hot_key = jax.random.fold_in(key, 12)
    favour = jax.random.randint(popular_key, (EXPERTS,), 0, 3).astype(jnp.int32)
    hottest = jax.random.randint(hot_key, (), 0, FLIGHT).astype(jnp.int32)
    expert_of_slot = jnp.arange(slot_total, dtype=jnp.int32) // CAP
    preference = favour[expert_of_slot] * 1024 + jnp.where(expert_of_slot == hottest, 8192, 0).astype(jnp.int32)

    def one_block(block_key):
        subkeys = jax.random.split(block_key, 3)
        jitter = jax.random.randint(subkeys[0], (slot_total,), 0, 4096).astype(jnp.int32)
        ranking = (jitter + preference) * slot_total + jnp.arange(slot_total, dtype=jnp.int32)
        chosen = jnp.argsort(-ranking)[:TOK_DEV * TOP]
        ordered = jnp.sort(expert_of_slot[chosen])
        layout_table = ordered.reshape(TOP, TOK_DEV).T
        layout_table = layout_table[jax.random.permutation(subkeys[1], TOK_DEV)]
        shuffle = jax.random.randint(subkeys[2], (TOK_DEV, TOP), 0, 1024).astype(jnp.int32) * TOP + jnp.arange(TOP, dtype=jnp.int32)[None, :]
        return jnp.take_along_axis(layout_table, jnp.argsort(shuffle, axis=1), axis=1)
    blocks = jax.vmap(one_block)(jax.random.split(key, block_count))
    return blocks.reshape(TOKENS, TOP).astype(jnp.int32)


def plant(values, rng, least, high):
    longest = values.shape.index(max(values.shape))
    spots = []
    for shift in (0, 1):
        where = [jax.random.randint(jax.random.fold_in(rng, axis), (), 0, length) for axis, length in enumerate(values.shape)]
        where[longest] = (where[longest] + shift) % values.shape[longest]
        spots.append(tuple(where))
    return values.at[spots[0]].set(least).at[spots[1]].set(high)


def steps_of(stream_key, dims, pieces, low, largest):
    factor_of = 1.0
    for position, parts in pieces:
        heights = jax.random.uniform(jax.random.fold_in(jax.random.fold_in(stream_key, 6), position), (parts,), jnp.float32, low / len(pieces), largest / len(pieces))
        factor_of = factor_of * jnp.repeat(jnp.exp(heights), dims[position] // parts).reshape((-1,) + (1,) * (len(dims) - 1 - position))
    return factor_of


def centred(rng, shape, deviation, most, cuts=(), kind=jnp.bfloat16):
    gain = steps_of(rng, shape, cuts, -0.22, 0.18) if cuts else 1.0
    values = jax.random.normal(rng, shape, jnp.float32) * deviation * gain
    return jnp.minimum(jnp.maximum(values, -most), most).astype(kind)


def setup_inputs(seed: int = 0) -> dict:
    key_list = jax.random.split(jax.random.key(seed), 6)
    tokens = centred(key_list[0], (TOKENS, D), 1.0, 6.0, ((0, 64), (1, 8)))
    route_ids = draw_route_ids(jax.random.fold_in(key_list[5], 71), 0)
    route_weight = jnp.clip(0.1 + 2.4 * jax.random.uniform(key_list[2], (TOKENS, TOP), jnp.float32) ** steps_of(key_list[2], (TOKENS, TOP), ((0, 64),), -0.2, 0.2), 0.1, 2.5)
    gate_up = centred(key_list[3], (FLIGHT, 2, D, FF), D ** -0.5, 0.0625, ((0, 64), (3, 8)))
    block_keep = plant((jax.random.randint(key_list[4], (FLIGHT, 2, D // BLOCK, FF // BLOCK), 0, 2) < 1).astype(jnp.int32), jax.random.fold_in(key_list[4], 1), 0, 1)
    return dict(tokens=tokens, route_ids=route_ids, route_weight=route_weight, gate_up=gate_up, block_keep=block_keep)


def expand_mask(keep_mask, block_size):
    widened = jnp.repeat(keep_mask, block_size, axis=1)
    return jnp.repeat(widened, block_size, axis=2)


def slot_table(picked, rounded, flight, capacity):
    token_count, pick_count = picked.shape
    flattened = picked.reshape(-1).astype(jnp.int32)
    matches = (flattened[:, None] == jnp.arange(flight, dtype=jnp.int32)[None, :]).astype(jnp.int32)
    before = (jnp.cumsum(matches, axis=0) - matches).astype(jnp.int32)
    slot_rank = jnp.sum(before * matches, axis=1).astype(jnp.int32)
    in_window = flattened < flight
    target = jnp.where(in_window, flattened * capacity + slot_rank, flight * capacity).astype(jnp.int32)
    source_row = (jnp.arange(token_count * pick_count, dtype=jnp.int32) // pick_count).astype(jnp.int32)
    token_of = jnp.full((flight * capacity,), -1, jnp.int32).at[target].set(source_row, mode="drop")
    weight_of = jnp.zeros((flight * capacity,), rounded.dtype).at[target].set(rounded.reshape(-1), mode="drop")
    return token_of, weight_of


def reference(tokens, route_ids, route_weight, gate_up, block_keep):
    flight = FLIGHT
    rounded = route_weight.astype(jnp.bfloat16)
    block_ids = route_ids.reshape(-1, TOK_DEV, TOP)
    block_weights = rounded.reshape(-1, TOK_DEV, TOP)
    token_of, weight_of = jax.vmap(lambda picked, scaling: slot_table(picked, scaling, flight, CAP))(block_ids, block_weights)
    block_count = block_ids.shape[0]
    offsets = (jnp.arange(block_count, dtype=jnp.int32) * TOK_DEV)[:, None]
    global_index = jnp.where(token_of >= 0, token_of + offsets, -1).astype(jnp.int32)
    global_index = global_index.reshape(block_count, flight, CAP).transpose(1, 0, 2).reshape(flight, ROWS)
    slot_weight = weight_of.reshape(block_count, flight, CAP).transpose(1, 0, 2).reshape(flight, ROWS)

    def one_expert(entries):
        source_index, scaling, matrices, keep_mask = entries
        filled = (source_index >= 0)[:, None]
        gathered = jnp.take(tokens, jnp.maximum(source_index, 0).astype(jnp.int32), axis=0)
        dispatched = jnp.where(filled, gathered, jnp.zeros((), tokens.dtype))
        masked = matrices * expand_mask(keep_mask, BLOCK).astype(matrices.dtype)
        gate_sums = jnp.dot(dispatched, masked[0], preferred_element_type=jnp.float32)
        up_sums = jnp.dot(dispatched, masked[1], preferred_element_type=jnp.float32)
        return (scaling.astype(jnp.float32)[:, None] * jax.nn.silu(gate_sums) * up_sums).astype(jnp.bfloat16)

    return lax.map(one_expert, (global_index, slot_weight, gate_up, block_keep))
```

```python
import functools

import jax
import jax.numpy as jnp
from jax import lax
from jax.experimental import pallas as pl
from jax.experimental.pallas import tpu as pltpu
from jax.sharding import PartitionSpec as P

BLOCK = 64
CAP = 8
MESH = pl.DeviceIdType.MESH
ZS, XS, YS, CS = 16, 4, 4, 2
HALF = 64


def kernel(dims, tok_ref, ids_ref, rw_ref, keep_ref, gu_ref, out_ref,
           zb, mb, xs, ws, wr, act, wraw, wm, maskv, res,
           z_s, z_r, m_s, m_r, x_s, x_r, w_s, w_r,
           y_s, y_r, h_s, h_r, c_s, c_r, l_sem):
    Z, X, Y, C = dims
    U = Z // 2
    T, F = tok_ref.shape
    D = F * Y * C
    H = out_ref.shape[1]
    NB = D // BLOCK
    XH = X // 2
    f32, bf16 = jnp.float32, jnp.bfloat16

    e = lax.axis_index("expert")
    t = lax.axis_index("tensor")
    z, x = e // X, e % X
    y, c = t // C, t % C
    up, down = ((z + 1) % Z) * X + x, ((z + Z - 1) % Z) * X + x
    z_to = (up, down)
    yn, yp, yo = (y + 1) % Y, (y + Y - 1) % Y, (y + 2) % Y
    y_to = (yn * C + c, yp * C + c)
    sib = y * C + 1 - c

    def cols(yy, cc):
        return pl.ds(pl.multiple_of((yy * C + cc) * F, 128), F)

    barrier = pltpu.get_barrier_semaphore()
    partners = [(up, t), (down, t), (e, y_to[0]), (e, y_to[1]), (e, sib)]
    partners += [(z * X + (x + k) % X, t) for k in range(1, X)]
    for dev in partners:
        pl.semaphore_signal(barrier, inc=1, device_id=dev, device_id_type=MESH)
    w_copy = pltpu.make_async_copy(gu_ref, wraw, l_sem.at[0])
    w_copy.start()
    own_copy = pltpu.make_async_copy(tok_ref, zb.at[U - 1, 1], l_sem.at[1])
    own_copy.start()
    pl.semaphore_wait(barrier, len(partners))

    TH = T // 2

    def z_copy(src, unit, d, h, slot):
        return pltpu.make_async_remote_copy(
            src_ref=src, dst_ref=zb.at[unit, slot, pl.ds(h * TH, TH)],
            send_sem=z_s.at[unit, d, h], recv_sem=z_r.at[unit, d, h],
            device_id=(z_to[d], t), device_id_type=MESH)

    def m_copy(src, unit, d, slot):
        return pltpu.make_async_remote_copy(
            src_ref=src, dst_ref=mb.at[unit, slot],
            send_sem=m_s.at[unit, d], recv_sem=m_r.at[unit, d],
            device_id=(z_to[d], t), device_id_type=MESH)

    for h in range(2):
        for d in range(2):
            z_copy(tok_ref.at[pl.ds(h * TH, TH)], 0, d, h, d).start()

    lane = lax.broadcasted_iota(jnp.int32, (T, 128), 1)
    row = lax.broadcasted_iota(jnp.int32, (T, 128), 0)
    lane_e = lane % HALF
    ids = ids_ref[...]
    rw = rw_ref[...].astype(bf16).astype(f32)
    hit = jnp.zeros((T, 128), f32)
    val = jnp.zeros((T, 128), f32)
    for k in range(ids.shape[1]):
        eq = ids[:, k:k + 1] == lane_e
        hit = jnp.where(eq, 1.0, hit)
        val = jnp.where(eq, rw[:, k:k + 1], val)
    tri = (lax.broadcasted_iota(jnp.int32, (T, T), 1)
           < lax.broadcasted_iota(jnp.int32, (T, T), 0))
    rank = jnp.dot(tri.astype(f32).astype(bf16), hit.astype(bf16), preferred_element_type=f32)
    rank = jnp.where(hit > 0.5, rank, -1.0)
    val = jnp.where(lane < HALF, (row + 1).astype(f32), val)
    sub8 = lax.broadcasted_iota(jnp.int32, (CAP, 128), 0)
    lane8 = lax.broadcasted_iota(jnp.int32, (CAP, 128), 1)
    meta = jnp.zeros((CAP, 128), f32)
    for k in range(CAP):
        total = jnp.sum(jnp.where(rank == float(k), val, 0.0), axis=0, keepdims=True)
        meta = jnp.where(sub8 == k, total, meta)
    mb[U - 1, 1] = meta

    keep = keep_ref[...].astype(f32)
    klane = lax.broadcasted_iota(jnp.int32, (2 * NB, 128), 1)
    maskv[...] = jnp.where(klane < BLOCK, keep[:, 0:1], keep[:, 1:2])
    for d in range(2):
        m_copy(mb.at[U - 1, 1], 0, d, d).start()

    w_copy.wait()

    def mask_block(b, carry):
        start = pl.multiple_of(b * BLOCK, BLOCK)
        for k in range(2):
            line = maskv[pl.ds(k * NB + b, 1), :].astype(bf16)
            wm[pl.ds(start, BLOCK), k * H:(k + 1) * H] = wraw[k, pl.ds(start, BLOCK), :] * line
        return carry

    lax.fori_loop(0, NB, mask_block, 0)
    own_copy.wait()

    def x_copies(u, k):
        to = (x + k) % X
        dev = (z * X + to, t)
        return (
            pltpu.make_async_remote_copy(
                src_ref=xs.at[u, to], dst_ref=act.at[u, x, :, cols(y, c)],
                send_sem=x_s.at[u, k - 1], recv_sem=x_r.at[u, k - 1],
                device_id=dev, device_id_type=MESH),
            pltpu.make_async_remote_copy(
                src_ref=ws.at[u, to], dst_ref=wr.at[u, x],
                send_sem=w_s.at[u, k - 1], recv_sem=w_r.at[u, k - 1],
                device_id=dev, device_id_type=MESH))

    def x_local(u):
        return (pltpu.make_async_copy(xs.at[u, x], act.at[u, x, :, cols(y, c)], l_sem.at[2 + u]),
                pltpu.make_async_copy(ws.at[u, x], wr.at[u, x], l_sem.at[2 + U + u]))

    def x_wait_recv(u, k):
        frm = (x + X - k) % X
        dev = (z * X + frm, t)
        for src, dst, s, r in ((xs.at[u, frm], act.at[u, frm, :, cols(y, c)], x_s, x_r),
                               (ws.at[u, frm], wr.at[u, frm], w_s, w_r)):
            pltpu.make_async_remote_copy(
                src_ref=src, dst_ref=dst, send_sem=s.at[u, k - 1], recv_sem=r.at[u, k - 1],
                device_id=dev, device_id_type=MESH).wait_recv()

    def y_copy(u, d, yy):
        ref = act.at[u, :, :, cols(yy, c)]
        return pltpu.make_async_remote_copy(
            src_ref=ref, dst_ref=ref, send_sem=y_s.at[u, d], recv_sem=y_r.at[u, d],
            device_id=(e, y_to[d]), device_id_type=MESH)

    def h_copy(u, d, yy):
        ref = act.at[u, pl.ds(d * XH, XH), :, cols(yy, c)]
        return pltpu.make_async_remote_copy(
            src_ref=ref, dst_ref=ref, send_sem=h_s.at[u, d], recv_sem=h_r.at[u, d],
            device_id=(e, y_to[d]), device_id_type=MESH)

    def c_copy(u, j, yy, cc):
        ref = act.at[u, :, :, cols(yy, cc)]
        return pltpu.make_async_remote_copy(
            src_ref=ref, dst_ref=ref, send_sem=c_s.at[u, j], recv_sem=c_r.at[u, j],
            device_id=(e, sib), device_id_type=MESH)

    def select(u):
        zero = jnp.zeros((CAP, T), f32)
        hots, weights = [], []
        for xx in range(X):
            for d in range(2):
                m = mb[u, d]
                want = z * X + xx
                tok = jnp.sum(jnp.where(lane8 == want, m, 0.0), axis=1, keepdims=True)
                wgt = jnp.sum(jnp.where(lane8 == want + HALF, m, 0.0), axis=1, keepdims=True)
                hot = jnp.where(tok == (lane8 + 1).astype(f32), 1.0, 0.0)
                hots.append(jnp.concatenate([hot, zero] if d == 0 else [zero, hot], axis=1))
                weights.append(jnp.broadcast_to(wgt, (CAP, 128)))
        hot = jnp.concatenate(hots, axis=0).astype(bf16)
        picked = jnp.dot(hot, zb[u].reshape(2 * T, F), preferred_element_type=f32)
        xs[u] = picked.astype(bf16).reshape(X, 2 * CAP, F)
        ws[u] = jnp.concatenate(weights, axis=0).astype(bf16).reshape(X, 2 * CAP, 128)

    def multiply(u):
        acc = jnp.dot(act[u].reshape(X * 2 * CAP, D), wm[...], preferred_element_type=f32)
        gate, upp = acc[:, :H], acc[:, H:]
        scale = wr[u].reshape(X * 2 * CAP, 128).astype(f32)
        hid = scale * (gate / (1.0 + jnp.exp(-gate))) * upp
        near, far = (z + Z - (u + 1)) % Z, (z + (u + 1) % U) % Z
        for xx in range(X):
            for d in range(2):
                s = (near if d == 0 else far) * X + xx
                r = (xx * 2 + d) * CAP
                res[pl.ds(pl.multiple_of(s * CAP, CAP), CAP), :] = hid[r:r + CAP]

    def step(i, carry):
        @pl.when(i < U - 1)
        def _():
            for d in range(2):
                z_copy(zb.at[i, d, pl.ds(0, TH)], i, d, 0, d).wait_recv()

                @pl.when(i < U - 2)
                def _():
                    z_copy(zb.at[i, d, pl.ds(0, TH)], i + 1, d, 0, d).start()
            for d in range(2):
                m_copy(mb.at[i, d], i, d, d).wait_recv()

                @pl.when(i < U - 2)
                def _():
                    m_copy(mb.at[i, d], i + 1, d, d).start()

        @pl.when(i == U - 2)
        def _():
            z_copy(zb.at[U - 2, 0, pl.ds(0, TH)], U - 1, 0, 0, 0).start()
            m_copy(mb.at[U - 2, 0], U - 1, 0, 0).start()

        @pl.when((i >= 1) & (i < U + 1))
        def _():
            u = i - 1
            for copy in x_local(u):
                copy.wait()
            for k in range(1, X):
                x_wait_recv(u, k)
            for d in range(2):
                y_copy(u, d, y).start()
            c_copy(u, 0, y, c).start()

        @pl.when((i >= 2) & (i < U + 2))
        def _():
            u = i - 2
            for d in range(2):
                yy = yp if d == 0 else yn
                y_copy(u, d, yy).wait_recv()
                h_copy(u, d, yy).start()
                c_copy(u, 1 + d, yy, c).start()

        @pl.when((i >= 3) & (i < U + 3))
        def _():
            u = i - 3
            for d in range(2):
                h_copy(u, d, yo).wait_recv()
            c_copy(u, 3, yo, c).start()

        @pl.when(i < U - 1)
        def _():
            for d in range(2):
                z_copy(zb.at[i, d, pl.ds(TH, TH)], i, d, 1, d).wait_recv()

                @pl.when(i < U - 2)
                def _():
                    z_copy(zb.at[i, d, pl.ds(TH, TH)], i + 1, d, 1, d).start()

        @pl.when(i == U - 2)
        def _():
            z_copy(zb.at[U - 2, 1, pl.ds(TH, TH)], U - 1, 1, 1, 0).start()

        @pl.when(i == U - 1)
        def _():
            z_copy(zb.at[U - 1, 0, pl.ds(0, TH)], U - 1, 0, 0, 0).wait_recv()
            m_copy(mb.at[U - 1, 0], U - 1, 0, 0).wait_recv()
            z_copy(zb.at[U - 1, 0, pl.ds(TH, TH)], U - 1, 1, 1, 0).wait_recv()

        @pl.when(i < U)
        def _():
            select(i)
            for k in range(1, X):
                for copy in x_copies(i, k):
                    copy.start()
            for copy in x_local(i):
                copy.start()

        @pl.when(i >= 4)
        def _():
            u = i - 4
            for j, yy in enumerate((y, yp, yn, yo)):
                c_copy(u, j, yy, 1 - c).wait_recv()
            multiply(u)

        return carry

    lax.fori_loop(0, U + 4, step, 0)

    def drain(u, carry):
        @pl.when(u < U - 1)
        def _():
            for d in range(2):
                m_copy(mb.at[u, d], u, d, d).wait_send()
                for h in range(2):
                    z_copy(zb.at[u, d, pl.ds(h * TH, TH)], u, d, h, d).wait_send()
        for k in range(1, X):
            for copy in x_copies(u, k):
                copy.wait_send()
        for d in range(2):
            y_copy(u, d, y).wait_send()
            h_copy(u, d, yo).wait_send()
        for j in range(4):
            c_copy(u, j, y, c).wait_send()
        return carry

    lax.fori_loop(0, U, drain, 0)
    z_copy(zb.at[U - 1, 0, pl.ds(0, TH)], U - 1, 0, 0, 0).wait_send()
    z_copy(zb.at[U - 1, 0, pl.ds(TH, TH)], U - 1, 1, 1, 0).wait_send()
    m_copy(mb.at[U - 1, 0], U - 1, 0, 0).wait_send()
    out_ref[...] = res[...].astype(out_ref.dtype)


def shards(dims, tokens, route_ids, route_weight, gate_up, block_keep):
    Z, X, Y, C = dims
    U = Z // 2
    T, F = tokens.shape
    D = F * Y * C
    H = gate_up.shape[3]
    NB = D // BLOCK
    bf16, f32 = jnp.bfloat16, jnp.float32
    dma = pltpu.SemaphoreType.DMA
    vmem = pl.BlockSpec(memory_space=pltpu.VMEM)
    hbm = pl.BlockSpec(memory_space=pl.ANY)
    out = pl.pallas_call(
        functools.partial(kernel, dims),
        out_shape=jax.ShapeDtypeStruct((Z * X * CAP, H), bf16),
        in_specs=[hbm, vmem, vmem, vmem, hbm],
        out_specs=vmem,
        scratch_shapes=[
            pltpu.VMEM((U, 2, T, F), bf16),
            pltpu.VMEM((U, 2, CAP, 128), f32),
            pltpu.VMEM((U, X, 2 * CAP, F), bf16),
            pltpu.VMEM((U, X, 2 * CAP, 128), bf16),
            pltpu.VMEM((U, X, 2 * CAP, 128), bf16),
            pltpu.VMEM((U, X, 2 * CAP, D), bf16),
            pltpu.VMEM((2, D, H), bf16),
            pltpu.VMEM((D, 2 * H), bf16),
            pltpu.VMEM((2 * NB, 128), f32),
            pltpu.VMEM((Z * X * CAP, H), f32),
            dma((U, 2, 2)), dma((U, 2, 2)),
            dma((U, 2)), dma((U, 2)),
            dma((U, X - 1)), dma((U, X - 1)),
            dma((U, X - 1)), dma((U, X - 1)),
            dma((U, 2)), dma((U, 2)),
            dma((U, 2)), dma((U, 2)),
            dma((U, 4)), dma((U, 4)),
            dma((2 + 2 * U,)),
        ],
        compiler_params=pltpu.CompilerParams(
            collective_id=0, has_side_effects=True, vmem_limit_bytes=56 * 1024 * 1024),
    )(tokens, route_ids, route_weight, block_keep.reshape(2 * NB, H // BLOCK), gate_up[0])
    return out.reshape(1, Z * X * CAP, H)


def build(mesh, dims):
    return jax.shard_map(
        functools.partial(shards, dims),
        mesh=mesh,
        in_specs=(
            P("expert", "tensor"),
            P("expert", None),
            P("expert", None),
            P("expert", None, None, "tensor"),
            P("expert", None, None, "tensor"),
        ),
        out_specs=P("expert", None, "tensor"),
        check_vma=False,
    )


def solution(mesh):
    return build(mesh, (ZS, XS, YS, CS))
```
